768 devices in a mesh: batch: 192 (over y_lo, z, x), rep: 4 (over y_hi, core).
Axes of the slice: x: 4, y: 8 (y_hi: 2, y_lo: 4; y = y_hi * 4 + y_lo), z: 12, core: 2. Of those that a mesh axis runs over, the one named last changes fastest.
Arguments:
- feats: bfloat16 [24576, 512], P('batch')
- partner: int32 [24576], P('batch'), may hold values from 0 to 24575, as said below
Outputs:
- grad: float32 [24576, 512], P('batch')
- loss: float32 [24576], P('batch')
The draws below stay inside these ranges and needn't reach their ends.
Inputs may be any that keep to these rules, and one draw needn't show every extreme that they name: partner pairs the rows: partner[partner[k]] = k and partner[k] != k.
All inputs are finite; a program needn't handle non-finite values.
Results may differ from the reference program's by a relative error of at most 0.0058.
Values may be sent and summed in bfloat16 or wider, within the bound.
A program may use at most 32 MiB of HBM per device.

```python
import math
import jax
import jax.numpy as jnp
from jax import lax

D = 512
EMBS = 24576


def pairing(key):
    return jax.random.permutation(jax.random.fold_in(key, 11), EMBS).astype(jnp.int32)


def draw_partner(key, part):
    order = pairing(key)
    half = EMBS // 2
    first = order[:half]
    second = order[half:]
    result = jnp.zeros((EMBS,), jnp.int32)
    result = result.at[first].set(second)
    result = result.at[second].set(first)
    return result


def draw_feats(key, part):
    order = pairing(key)
    half = EMBS // 2
    first = order[:half]
    second = order[half:]
    classes = max(1, EMBS // 32)
    key_center = jax.random.fold_in(key, 21)
    key_class = jax.random.fold_in(key, 26)
    key_image = jax.random.fold_in(key, 27)
    key_istd = jax.random.fold_in(key, 28)
    key_vstd = jax.random.fold_in(key, 22)
    key_left = jax.random.fold_in(key, 23)
    key_right = jax.random.fold_in(key, 24)
    key_scale = jax.random.fold_in(key, 25)
    label = jax.random.randint(key_class, (half,), 0, classes)
    image_std = jnp.exp(jax.random.uniform(key_istd, (half, 1), jnp.float32, jnp.log(0.4), jnp.log(1.2)))
    view_std = jnp.exp(jax.random.uniform(key_vstd, (half, 1), jnp.float32, jnp.log(0.3), jnp.log(0.9)))
    centers = jax.random.normal(key_center, (classes, D), jnp.float32)
    image_noise = jax.random.normal(key_image, (half, D), jnp.float32)
    left = jax.random.normal(key_left, (half, D), jnp.float32)
    right = jax.random.normal(key_right, (half, D), jnp.float32)
    shared = centers[label] + image_std * image_noise
    view_one = shared + view_std * left
    view_two = shared + view_std * right
    result = jnp.zeros((EMBS, D), jnp.float32)
    result = result.at[first].set(view_one)
    result = result.at[second].set(view_two)
    row_scale = jnp.exp(jax.random.uniform(key_scale, (EMBS, 1), jnp.float32, 0.0, jnp.log(10.0)))
    return (result * row_scale).astype(jnp.bfloat16)


def setup_inputs(seed: int = 0) -> dict:
    keys = jax.random.split(jax.random.key(seed), 3)
    return {
        "feats": draw_feats(jax.random.fold_in(keys[2], 71), 0),
        "partner": draw_partner(jax.random.fold_in(keys[2], 71), 0),
    }


inv_temp = 10.0

def reference(feats, partner):
    hf = feats.astype(jnp.float32)
    scale = lax.rsqrt(lax.optimization_barrier(jnp.sum(hf * hf, axis=-1, keepdims=True)) + 1e-06)
    unit = hf * scale
    embed = unit.astype(jnp.bfloat16)
    total = embed.shape[0]
    all_ids = jnp.arange(total, dtype=jnp.int32)
    span = math.gcd(total, 512)
    starts = jnp.arange(total // span, dtype=jnp.int32) * span

    def stats(start):
        block = lax.dynamic_slice_in_dim(embed, start, span, 0)
        mates = lax.dynamic_slice_in_dim(partner, start, span, 0)
        rows = start + jnp.arange(span, dtype=jnp.int32)
        score = jnp.dot(block, embed.T, preferred_element_type=jnp.float32) * inv_temp
        weight = jnp.where(all_ids[None, :] == rows[:, None], 0.0, jnp.exp(score - inv_temp))
        pscore = lax.optimization_barrier(jnp.sum(jnp.where(all_ids[None, :] == mates[:, None], score, 0.0), axis=1))
        return (lax.optimization_barrier(jnp.sum(weight, axis=1)), pscore)
    denom, pscore = lax.map(stats, starts)
    denom = denom.reshape(total)
    pscore = pscore.reshape(total)
    lse = jnp.log(denom) + inv_temp
    loss = lse - pscore

    def grad_rows(start):
        block = lax.dynamic_slice_in_dim(embed, start, span, 0)
        mates = lax.dynamic_slice_in_dim(partner, start, span, 0)
        own_lse = lax.dynamic_slice_in_dim(lse, start, span, 0)
        rows = start + jnp.arange(span, dtype=jnp.int32)
        score = jnp.dot(block, embed.T, preferred_element_type=jnp.float32) * inv_temp
        coeff = jnp.exp(score - own_lse[:, None]) + jnp.exp(score - lse[None, :])
        coeff = coeff - 2.0 * jnp.where(all_ids[None, :] == mates[:, None], 1.0, 0.0)
        coeff = jnp.where(all_ids[None, :] == rows[:, None], 0.0, coeff).astype(jnp.bfloat16)
        return jnp.dot(coeff, embed, preferred_element_type=jnp.float32) * inv_temp
    dz = lax.map(grad_rows, starts).reshape(total, embed.shape[1])
    grad = scale * (dz - unit * lax.optimization_barrier(jnp.sum(unit * dz, axis=-1, keepdims=True)))
    return (grad, loss)
```

```python
import jax
import jax.numpy as jnp
from jax import lax
from jax.experimental import pallas as pl
from jax.experimental.pallas import tpu as pltpu
from jax.sharding import PartitionSpec as P

MESH = pl.DeviceIdType.MESH
F32 = jnp.float32
BF16 = jnp.bfloat16

NX, NY, NZ = 4, 8, 12
NQ = 4
PLANE = NX * NQ
ROWS, WIDTH = 128, 512
HALF = ROWS // 2
NR = PLANE * HALF
TILE = 256


def kernel(
    feats_ref,
    partner_ref,
    grad_ref,
    loss_ref,
    rows,
    cols,
    colp,
    ebuf,
    dacc,
    pacc,
    rsend,
    rmsg,
    csend,
    cmsg,
    rcol,
    square,
    rrow,
    coeff,
    psend,
    prec,
    row_s,
    row_r,
    ring_s,
    ring_r,
    pair_s,
    pair_r,
    part_s,
    part_r,
    sum_s,
    sum_r,
    den_s,
    den_r,
    dz_s,
    dz_r,
    fin_s,
    fin_r,
):
    block = lax.axis_index("batch")
    layer = lax.axis_index("rep")
    x = block % NX
    z = (block // NX) % NZ
    q = block // (NX * NZ)
    core = layer % 2
    y = (layer // 2) * NQ + q
    mine = q * NX + x

    def device(dx, dy, dz, flip):
        ny = (y + dy) % NY
        nz = (z + dz) % NZ
        nx = (x + dx) % NX
        return ((ny % NQ) * (NX * NZ) + nz * NX + nx, (ny // NQ) * 2 + (core + flip) % 2)

    def y_step(dyi):
        return dyi + (dyi // 3) * 4 + (dyi // 2 - dyi // 3) * 4 * core

    def plane_dest(i):
        return device(i % NX, y_step(i // NX), 0, 0)

    def plane_source(i):
        return device(NX - i % NX, NY - y_step(i // NX), 0, 0)

    def plane_dest_slot(i):
        return ((q + i // NX) % NQ) * NX + (x + i % NX) % NX

    barrier = pltpu.get_barrier_semaphore()

    def greet_plane(i, carry):
        pl.semaphore_signal(barrier, inc=1, device_id=plane_source(i), device_id_type=MESH)
        return carry

    def greet_line(i, carry):
        pl.semaphore_signal(
            barrier, inc=1, device_id=device(0, 0, i // 2, i % 2), device_id_type=MESH
        )
        return carry

    lax.fori_loop(1, PLANE, greet_plane, 0)
    lax.fori_loop(1, 2 * NZ, greet_line, 0)

    hf = feats_ref[...].astype(F32)
    scale = lax.rsqrt(jnp.sum(hf * hf, axis=-1, keepdims=True) + 1e-06)
    embed = (hf * scale).astype(BF16)
    cols[z] = embed
    colp[z] = partner_ref[...]
    half = pl.multiple_of(core * HALF, HALF)
    rows[mine] = cols[z, pl.ds(half, HALF), :]

    pl.semaphore_wait(barrier, PLANE - 1 + 2 * NZ - 1)

    ahead = 1 + (NZ - 2) * core

    def ring_copy(k, h):
        src = (z + (NZ - ahead) * (k - 1)) % NZ
        part = cols.at[src, pl.ds(h * HALF, HALF)]
        n = (k - 1) * 2 + h
        return pltpu.make_async_remote_copy(
            src_ref=part,
            dst_ref=part,
            send_sem=ring_s.at[n],
            recv_sem=ring_r.at[n],
            device_id=device(0, 0, ahead, 0),
            device_id_type=MESH,
        )

    def ring_last():
        src = (z + (NZ - ahead) * (NZ // 2 - 1)) % NZ
        part = cols.at[src, pl.ds(half, HALF)]
        return pltpu.make_async_remote_copy(
            src_ref=part,
            dst_ref=part,
            send_sem=ring_s.at[10],
            recv_sem=ring_r.at[10],
            device_id=device(0, 0, ahead, 0),
            device_id_type=MESH,
        )

    def pair_copy(k, h, n):
        src = (z + (NZ - ahead) * k) % NZ
        part = cols.at[src, pl.ds(pl.multiple_of(h * HALF, HALF), HALF)]
        return pltpu.make_async_remote_copy(
            src_ref=part,
            dst_ref=part,
            send_sem=pair_s.at[n],
            recv_sem=pair_r.at[n],
            device_id=device(0, 0, 0, 1),
            device_id_type=MESH,
        )

    def row_copy(i):
        return pltpu.make_async_remote_copy(
            src_ref=cols.at[z, pl.ds(half, HALF)],
            dst_ref=rows.at[mine],
            send_sem=row_s.at[i],
            recv_sem=row_r.at[i],
            device_id=plane_dest(i),
            device_id_type=MESH,
        )

    def partner_copy(i):
        return pltpu.make_async_remote_copy(
            src_ref=partner_ref,
            dst_ref=colp.at[z],
            send_sem=part_s.at[i],
            recv_sem=part_r.at[i],
            device_id=device(0, 0, i, 0),
            device_id_type=MESH,
        )

    def start(make):
        def body(i, carry):
            make(i).start()
            return carry

        return body

    def wait_recv(make):
        def body(i, carry):
            make(i).wait_recv()
            return carry

        return body

    def wait_send(make):
        def body(i, carry):
            make(i).wait_send()
            return carry

        return body

    for h in range(2):
        ring_copy(1, h).start()
    lax.fori_loop(1, PLANE, start(row_copy), 0)
    lax.fori_loop(1, NZ, start(partner_copy), 0)

    for k in range(1, 6):
        for h in range(2):
            ring_copy(k, h).wait_recv()
            if k < 5:
                ring_copy(k + 1, h).start()
            pair_copy(k, h, (k - 1) * 2 + h).start()
    ring_last().start()
    lax.fori_loop(1, PLANE, wait_recv(row_copy), 0)
    lax.fori_loop(1, NZ, wait_recv(partner_copy), 0)
    ring_last().wait_recv()
    pair_copy(6, core, 10).start()
    for n in range(11):
        pair_copy(1, 0, n).wait_recv()

    lane = lax.broadcasted_iota(jnp.int32, (1, TILE), 1)
    row_in_tile = lax.broadcasted_iota(jnp.int32, (TILE, 1), 0)

    def row_ids(t):
        return (t * NZ * NX + z * NX) * ROWS + core * HALF + (row_in_tile // HALF) * HALF + row_in_tile

    def mates(k):
        return jnp.concatenate([colp[2 * k], colp[2 * k + 1]], axis=1)

    dacc[...] = jnp.zeros_like(dacc)
    pacc[...] = jnp.zeros_like(pacc)

    def score_step(k, carry):
        keys = cols[pl.ds(2 * k, 2)].reshape(TILE, WIDTH)
        key_ids = (q * NZ * NX + (2 * k + lane // ROWS) * NX + x) * ROWS + lane % ROWS
        mate = mates(k)
        for t in range(NQ):
            ids = row_ids(t)
            span = pl.ds(t * TILE, TILE)
            score = lax.dot_general(
                rows[pl.ds(t * NX, NX)].reshape(TILE, WIDTH),
                keys,
                (((1,), (1,)), ((), ())),
                preferred_element_type=F32,
            ) * 10.0
            weight = jnp.where(key_ids == ids, 0.0, jnp.exp(score - 10.0))
            hits = jnp.where(mate == ids, score, 0.0)
            ebuf[k, span] = weight
            dacc[span] += weight[:, :ROWS] + weight[:, ROWS:]
            pacc[span] += hits[:, :ROWS] + hits[:, ROWS:]
        return carry

    lax.fori_loop(0, NZ // 2, score_step, 0)

    for g in range(8):
        span = pl.ds(g * ROWS, ROWS)
        rsend[pl.ds(g, 1)] = jnp.sum(dacc[span].T, axis=0, keepdims=True)
        rsend[pl.ds(8 + g, 1)] = jnp.sum(pacc[span].T, axis=0, keepdims=True)
    rmsg[mine] = rsend[...]

    def sum_copy(i):
        return pltpu.make_async_remote_copy(
            src_ref=rsend,
            dst_ref=rmsg.at[mine],
            send_sem=sum_s.at[i],
            recv_sem=sum_r.at[i],
            device_id=plane_dest(i),
            device_id_type=MESH,
        )

    lax.fori_loop(1, PLANE, start(sum_copy), 0)
    lax.fori_loop(1, PLANE, wait_recv(sum_copy), 0)
    total = rmsg[0]
    for p in range(1, PLANE):
        total = total + rmsg[p]
    square[pl.ds(0, 16)] = total

    low = lax.broadcasted_iota(jnp.int32, (1, ROWS), 1) < HALF
    own_den = square[pl.ds(mine // 2, 1)]
    own_pos = square[pl.ds(8 + mine // 2, 1)]
    odd = mine % 2 == 1
    own_den = jnp.where(odd, pltpu.roll(own_den, HALF, 1), own_den)
    own_pos = jnp.where(odd, own_pos, pltpu.roll(own_pos, HALF, 1))
    note = jnp.where(low, own_den, own_pos)
    csend[...] = note
    cmsg[2 * z + core] = note

    def den_copy(i):
        return pltpu.make_async_remote_copy(
            src_ref=csend,
            dst_ref=cmsg.at[2 * z + core],
            send_sem=den_s.at[i],
            recv_sem=den_r.at[i],
            device_id=device(0, 0, i // 2, i % 2),
            device_id_type=MESH,
        )

    lax.fori_loop(1, 2 * NZ, start(den_copy), 0)

    square[pl.ds(0, 8)] = 1.0 / total[:8]
    turned = square[...].T
    for g in range(8):
        rrow[pl.ds(g * ROWS, ROWS)] = jnp.broadcast_to(turned[:, g : g + 1], (ROWS, ROWS))

    lax.fori_loop(1, 2 * NZ, wait_recv(den_copy), 0)

    def den_of(j):
        return jnp.where(low, cmsg[2 * j], pltpu.roll(cmsg[2 * j + 1], HALF, 1))

    for j in range(NZ):
        rcol[j] = 1.0 / den_of(j)
    pos = jnp.where(low, pltpu.roll(cmsg[2 * z], HALF, 1), cmsg[2 * z + 1])
    loss_ref[...] = jnp.log(den_of(z)) + 10.0 - pos

    def dz_copy(i):
        return pltpu.make_async_remote_copy(
            src_ref=psend.at[plane_dest_slot(i)],
            dst_ref=prec.at[mine],
            send_sem=dz_s.at[i],
            recv_sem=dz_r.at[i],
            device_id=plane_dest(i),
            device_id_type=MESH,
        )

    keys_all = cols[...].reshape(NZ * ROWS, WIDTH)
    for turn in (2, 1, 3, 0):
        t = (q + turn) % NQ
        ids = row_ids(t)
        span = pl.ds(pl.multiple_of(t * TILE, TILE), TILE)
        row_part = rrow[span]
        row_part = jnp.concatenate([row_part, row_part], axis=1)

        def coeff_step(k, carry):
            col_part = jnp.concatenate([rcol[2 * k], rcol[2 * k + 1]], axis=1)
            value = ebuf[k, span] * (row_part + col_part)
            value = value - jnp.where(mates(k) == ids, 2.0, 0.0)
            coeff[:, pl.ds(pl.multiple_of(k * TILE, TILE), TILE)] = value.astype(BF16)
            return carry

        for k in range(NZ // 2):
            coeff_step(k, 0)
        dz = jnp.dot(coeff[...], keys_all, preferred_element_type=F32)
        psend[pl.ds(t * NX, NX)] = dz.astype(BF16).reshape(NX, HALF, WIDTH)
        if turn == 0:
            prec[mine] = psend[mine]
        lax.fori_loop(max(1, turn * NX), turn * NX + NX, start(dz_copy), 0)

    lax.fori_loop(1, PLANE, wait_recv(dz_copy), 0)
    acc = prec[0].astype(F32)
    for p in range(1, PLANE):
        acc = acc + prec[p].astype(F32)
    acc = acc * 10.0
    hf = feats_ref[pl.ds(half, HALF)].astype(F32)
    scale = lax.rsqrt(jnp.sum(hf * hf, axis=-1, keepdims=True) + 1e-06)
    unit = hf * scale
    grad_ref[pl.ds(half, HALF)] = scale * (acc - unit * jnp.sum(unit * acc, axis=-1, keepdims=True))
    part = grad_ref.at[pl.ds(half, HALF)]
    last = pltpu.make_async_remote_copy(
        src_ref=part,
        dst_ref=part,
        send_sem=fin_s,
        recv_sem=fin_r,
        device_id=device(0, 0, 0, 1),
        device_id_type=MESH,
    )
    last.start()

    for k in range(1, 6):
        for h in range(2):
            ring_copy(k, h).wait_send()
    ring_last().wait_send()
    for n in range(11):
        pair_copy(1, 0, n).wait_send()
    lax.fori_loop(1, PLANE, wait_send(row_copy), 0)
    lax.fori_loop(1, NZ, wait_send(partner_copy), 0)
    lax.fori_loop(1, PLANE, wait_send(sum_copy), 0)
    lax.fori_loop(1, 2 * NZ, wait_send(den_copy), 0)
    lax.fori_loop(1, PLANE, wait_send(dz_copy), 0)
    last.wait()


def on_device(feats, partner):
    vmem = pl.BlockSpec(memory_space=pltpu.VMEM)
    dma = pltpu.SemaphoreType.DMA
    grad, loss = pl.pallas_call(
        kernel,
        out_shape=(
            jax.ShapeDtypeStruct((ROWS, WIDTH), F32),
            jax.ShapeDtypeStruct((1, ROWS), F32),
        ),
        in_specs=[vmem, vmem],
        out_specs=(vmem, vmem),
        scratch_shapes=[
            pltpu.VMEM((PLANE, HALF, WIDTH), BF16),
            pltpu.VMEM((NZ, ROWS, WIDTH), BF16),
            pltpu.VMEM((NZ, 1, ROWS), jnp.int32),
            pltpu.VMEM((NZ // 2, NR, TILE), F32),
            pltpu.VMEM((NR, ROWS), F32),
            pltpu.VMEM((NR, ROWS), F32),
            pltpu.VMEM((16, ROWS), F32),
            pltpu.VMEM((PLANE, 16, ROWS), F32),
            pltpu.VMEM((1, ROWS), F32),
            pltpu.VMEM((2 * NZ, 1, ROWS), F32),
            pltpu.VMEM((NZ, 1, ROWS), F32),
            pltpu.VMEM((ROWS, ROWS), F32),
            pltpu.VMEM((NR, ROWS), F32),
            pltpu.VMEM((TILE, NZ * ROWS), BF16),
            pltpu.VMEM((PLANE, HALF, WIDTH), BF16),
            pltpu.VMEM((PLANE, HALF, WIDTH), BF16),
            dma((PLANE,)),
            dma((PLANE,)),
            dma((11,)),
            dma((11,)),
            dma((11,)),
            dma((11,)),
            dma((NZ,)),
            dma((NZ,)),
            dma((PLANE,)),
            dma((PLANE,)),
            dma((2 * NZ,)),
            dma((2 * NZ,)),
            dma((PLANE,)),
            dma((PLANE,)),
            dma,
            dma,
        ],
        compiler_params=pltpu.CompilerParams(
            collective_id=0, has_side_effects=True, vmem_limit_bytes=48 * 2**20
        ),
    )(feats, partner.reshape(1, ROWS))
    return grad, loss.reshape(ROWS)


def solution(mesh):
    in_specs = (P("batch", None), P("batch"))
    out_specs = (P("batch", None), P("batch"))
    return jax.shard_map(
        on_device, mesh=mesh, in_specs=in_specs, out_specs=out_specs, check_vma=False
    )
```

```python
import jax
import jax.numpy as jnp
from jax import lax
from jax.experimental import pallas as pl
from jax.experimental.pallas import tpu as pltpu
from jax.sharding import PartitionSpec as P

MESH = pl.DeviceIdType.MESH
F32 = jnp.float32
BF16 = jnp.bfloat16

NX, NY, NZ = 4, 8, 12
NQ = 4
PLANE = NX * NQ
ROWS, WIDTH = 128, 512
HALF = ROWS // 2
NR = PLANE * HALF
TILE = 256
CHUNKS = 4
CHUNK = ROWS // CHUNKS
NEAR = 9


def kernel(
    feats_hbm,
    partner_hbm,
    grad_ref,
    loss_ref,
    feats,
    rows,
    cols,
    colp,
    ebuf,
    dacc,
    rsend,
    rmsg,
    csend,
    cmsg,
    ssend,
    smsg,
    rcol,
    square,
    rrow,
    coeff,
    psend,
    prec,
    in_sem,
    row_s,
    row_r,
    ring_s,
    ring_r,
    pair_s,
    pair_r,
    part_s,
    part_r,
    sum_s,
    sum_r,
    near_s,
    near_r,
    far_s,
    far_r,
    pos_s,
    pos_r,
    dz_s,
    dz_r,
    fin_s,
    fin_r,
):
    block = lax.axis_index("batch")
    layer = lax.axis_index("rep")
    x = block % NX
    z = (block // NX) % NZ
    q = block // (NX * NZ)
    core = layer % 2
    y = (layer // 2) * NQ + q
    mine = q * NX + x

    def device(dx, dy, dz, flip):
        ny = (y + dy) % NY
        nz = (z + dz) % NZ
        nx = (x + dx) % NX
        return ((ny % NQ) * (NX * NZ) + nz * NX + nx, (ny // NQ) * 2 + (core + flip) % 2)

    def remote(src, dst, send_sem, recv_sem, target):
        return pltpu.make_async_remote_copy(
            src_ref=src,
            dst_ref=dst,
            send_sem=send_sem,
            recv_sem=recv_sem,
            device_id=target,
            device_id_type=MESH,
        )

    def y_step(dyi):
        return dyi + (dyi // 3) * 4 + (dyi // 2 - dyi // 3) * 4 * core

    def plane_dest(i):
        return device(i % NX, y_step(i // NX), 0, 0)

    def plane_source(i):
        return device(NX - i % NX, NY - y_step(i // NX), 0, 0)

    def plane_dest_slot(i):
        return ((q + i // NX) % NQ) * NX + (x + i % NX) % NX

    def line_dest(i):
        return device(0, 0, i // 2, i % 2)

    fetch = [
        pltpu.make_async_copy(feats_hbm, feats, in_sem.at[0]),
        pltpu.make_async_copy(partner_hbm, colp.at[0], in_sem.at[1]),
    ]
    for copy in fetch:
        copy.start()

    barrier = pltpu.get_barrier_semaphore()

    def greet_plane(i, carry):
        pl.semaphore_signal(barrier, inc=1, device_id=plane_source(i), device_id_type=MESH)
        return carry

    ahead = 1 + (NZ - 2) * core
    for dz, flip in ((NZ - ahead, 0), (ahead, 1), (0, 1)):
        pl.semaphore_signal(
            barrier, inc=1, device_id=device(0, 0, dz, flip), device_id_type=MESH
        )
    lax.fori_loop(1, PLANE, greet_plane, 0)
    for copy in fetch:
        copy.wait()

    hf = feats[...].astype(F32)
    scale = lax.rsqrt(jnp.sum(hf * hf, axis=-1, keepdims=True) + 1e-06)
    embed = (hf * scale).astype(BF16)
    cols[0] = embed
    half = pl.multiple_of(core * HALF, HALF)
    rows[mine] = cols[0, pl.ds(half, HALF), :]

    pl.semaphore_wait(barrier, PLANE - 1 + 3)

    LAST = NZ // 2

    def ring_slot(k):
        if k == 0:
            return 0
        return 1 if k == LAST else 2 * k + 1 - core

    def chunk_rows(h):
        return pl.ds(pl.multiple_of((2 * core + h) % CHUNKS * CHUNK, CHUNK), CHUNK)

    def ring_copy(k, h):
        n = (k - 1) * CHUNKS + h
        target = device(0, 0, ahead, 0)
        if k == LAST:
            target = device(0, 0, ahead, h // 2)
            h = h % 2
        return remote(
            cols.at[ring_slot(k - 1), chunk_rows(h)],
            cols.at[ring_slot(k), chunk_rows(h)],
            ring_s.at[n],
            ring_r.at[n],
            target,
        )

    def pair_copy(k):
        part = cols.at[ring_slot(k)]
        return remote(part, part, pair_s.at[k - 1], pair_r.at[k - 1], device(0, 0, 0, 1))

    def mate_copy(k):
        return remote(
            colp.at[ring_slot(k - 1)],
            colp.at[ring_slot(k)],
            part_s.at[k - 1],
            part_r.at[k - 1],
            device(0, 0, ahead, 0),
        )

    def mate_pair_copy(k):
        part = colp.at[ring_slot(k)]
        return remote(part, part, part_s.at[5 + k], part_r.at[5 + k], device(0, 0, 0, 1))

    def row_copy(i):
        return remote(
            cols.at[0, pl.ds(half, HALF)], rows.at[mine], row_s.at[i], row_r.at[i], plane_dest(i)
        )

    def slot_of(off):
        off = off % NZ
        if off in (0, LAST):
            return off // LAST
        return 2 * off if off < LAST else 2 * (NZ - off) + 1

    def loop(lo, hi, act):
        def body(i, carry):
            act(i)
            return carry

        lax.fori_loop(lo, hi, body, 0)

    pending = []

    def finish():
        for settle in pending:
            settle()

    for h in range(CHUNKS):
        ring_copy(1, h).start()
    mate_copy(1).start()
    for dyi in (0, 1, 3, 2):
        loop(max(1, dyi * NX), dyi * NX + NX, lambda i: row_copy(i).start())

    def settle_gather():
        for k in range(1, LAST + 1):
            for h in range(CHUNKS):
                ring_copy(k, h).wait_send()
            mate_copy(k).wait_send()
            if k < LAST:
                pair_copy(k).wait_send()
                mate_pair_copy(k).wait_send()
        loop(1, PLANE, lambda i: row_copy(i).wait_send())

    pending.append(settle_gather)

    def ring_step(k):
        for h in range(CHUNKS):
            ring_copy(k, h).wait_recv()
            if k < LAST - 1:
                ring_copy(k + 1, h).start()
            elif k == LAST - 1 and h < CHUNKS // 2:
                ring_copy(k + 1, h).start()
                ring_copy(k + 1, h + 2).start()
        mate_copy(k).wait_recv()
        if k < LAST:
            mate_copy(k + 1).start()
            pair_copy(k).start()
            mate_pair_copy(k).start()

    def pair_in(k):
        pair_copy(k).wait_recv()
        mate_pair_copy(k).wait_recv()

    def rows_in(turn):
        dyi = (NQ - turn) % NQ
        loop(max(1, dyi * NX), dyi * NX + NX, lambda i: row_copy(i).wait_recv())

    lane = lax.broadcasted_iota(jnp.int32, (1, ROWS), 1)
    row_in_tile = lax.broadcasted_iota(jnp.int32, (TILE, 1), 0)

    def row_ids(t):
        return (t * NZ * NX + z * NX) * ROWS + core * HALF + (row_in_tile // HALF) * HALF + row_in_tile

    def mates(j):
        return jnp.concatenate([colp[2 * j], colp[2 * j + 1]], axis=1)

    def score_of(t, keys):
        return lax.dot_general(
            rows[pl.ds(t * NX, NX)].reshape(TILE, WIDTH),
            keys,
            (((1,), (1,)), ((), ())),
            preferred_element_type=F32,
        ) * 10.0

    def place(slot):
        return slot - 1 if slot > 1 else slot * (NZ - 1)

    def sums(turn, slot, weight, hits):
        weight = jnp.sum(weight, axis=0, keepdims=True)
        hits = jnp.sum(hits, axis=0, keepdims=True)
        if turn == 0:
            csend[place(slot)] = weight
            ssend[place(slot)] = hits
        else:
            csend[place(slot)] += weight
            ssend[place(slot)] += hits

    def single(turn, slot):
        t = (q + turn) % NQ
        ids = row_ids(t)
        span = pl.ds(pl.multiple_of(t * TILE, TILE), TILE)
        score = score_of(t, cols[slot])
        weight = jnp.exp(score - 10.0)
        if slot == 0 and turn == 0:
            key_ids = block * ROWS + lane
            weight = jnp.where(key_ids == ids, 0.0, weight)
        hits = jnp.where(colp[slot] == ids, score, 0.0)
        ebuf[0, span, slot * ROWS : slot * ROWS + ROWS] = weight
        if slot == 0:
            dacc[span] = weight
        else:
            dacc[span] += weight
        sums(turn, slot, weight, hits)

    def pair(turn, j):
        t = (q + turn) % NQ
        ids = row_ids(t)
        span = pl.ds(pl.multiple_of(t * TILE, TILE), TILE)
        score = score_of(t, cols[2 * j : 2 * j + 2].reshape(TILE, WIDTH))
        weight = jnp.exp(score - 10.0)
        hits = jnp.where(mates(j) == ids, score, 0.0)
        ebuf[j, span] = weight
        dacc[span] += weight[:, :ROWS] + weight[:, ROWS:]
        for side in range(2):
            cut = slice(side * ROWS, side * ROWS + ROWS)
            sums(turn, 2 * j + side, weight[:, cut], hits[:, cut])

    def near_copy(i):
        return remote(
            csend.at[pl.ds(0, NEAR)],
            cmsg.at[i // 2 * 2 + core, pl.ds(0, NEAR)],
            near_s.at[i],
            near_r.at[i],
            line_dest(i),
        )

    def far_copy(i):
        return remote(
            csend.at[pl.ds(NEAR, NZ - NEAR)],
            cmsg.at[i // 2 * 2 + core, pl.ds(NEAR, NZ - NEAR)],
            far_s.at[i],
            far_r.at[i],
            line_dest(i),
        )

    ring_step(1)
    ring_step(2)
    ring_step(3)
    rows_in(0)
    single(0, 0)
    pair_in(1)
    pair(0, 1)
    pair_in(2)
    pair(0, 2)
    ring_step(4)
    rows_in(3)
    rows_in(1)
    for turn in (1, 3):
        single(turn, 0)
        pair(turn, 1)
    pair_in(3)
    pair(0, 3)
    ring_step(5)
    for turn in (1, 3):
        pair(turn, 2)
        pair(turn, 3)
    pair_in(4)
    for turn in (0, 1, 3):
        pair(turn, 4)
    rows_in(2)
    single(2, 0)
    for j in range(1, 5):
        pair(2, j)
    pair_in(5)
    pair(0, 5)
    pair(1, 5)
    ring_step(6)
    loop(1, 2 * NZ, lambda i: near_copy(i).start())
    pending.append(lambda: loop(1, 2 * NZ, lambda i: near_copy(i).wait_send()))
    pair(2, 5)
    pair(3, 5)
    for turn in range(NQ):
        single(turn, 1)

    loop(1, 2 * NZ, lambda i: far_copy(i).start())
    pending.append(lambda: loop(1, 2 * NZ, lambda i: far_copy(i).wait_send()))

    for g in range(8):
        span = pl.ds(g * ROWS, ROWS)
        rsend[pl.ds(g, 1)] = jnp.sum(dacc[span].T, axis=0, keepdims=True)

    def sum_copy(i):
        return remote(rsend, rmsg.at[mine], sum_s.at[i], sum_r.at[i], plane_dest(i))

    loop(1, PLANE, lambda i: sum_copy(i).start())
    pending.append(lambda: loop(1, PLANE, lambda i: sum_copy(i).wait_send()))

    def pos_copy(d, flip):
        n = 2 * d + flip
        return remote(
            ssend.at[place(slot_of(d))],
            smsg.at[2 * d + core],
            pos_s.at[n],
            pos_r.at[n],
            device(0, 0, d, flip),
        )

    others = [(d, flip) for d in range(NZ) for flip in range(2) if d + flip]
    for d, flip in others:
        pos_copy(d, flip).start()
    pending.append(lambda: [pos_copy(d, flip).wait_send() for d, flip in others])

    rmsg[mine] = rsend[...]
    cmsg[core] = csend[...]
    smsg[core] = ssend[0]
    loop(1, PLANE, lambda i: sum_copy(i).wait_recv())
    total = rmsg[0]
    for p in range(1, PLANE):
        total = total + rmsg[p]
    square[pl.ds(0, 8)] = 1.0 / total
    turned = square[...].T
    for g in range(8):
        rrow[pl.ds(g * ROWS, ROWS)] = jnp.broadcast_to(turned[:, g : g + 1], (ROWS, ROWS))

    loop(1, 2 * NZ, lambda i: near_copy(i).wait_recv())
    loop(1, 2 * NZ, lambda i: far_copy(i).wait_recv())
    own_den = None
    for off in range(NZ):
        den = None
        for d in range(NZ):
            for c in range(2):
                part = cmsg[2 * d + c, place(slot_of(off + d))]
                den = part if den is None else den + part
        rcol[slot_of(off)] = 1.0 / den
        if off == 0:
            own_den = den
    loss_ref[...] = jnp.log(own_den) + 10.0

    def dz_copy(i):
        return remote(
            psend.at[plane_dest_slot(i)], prec.at[mine], dz_s.at[i], dz_r.at[i], plane_dest(i)
        )

    keys_all = cols[...].reshape(NZ * ROWS, WIDTH)
    for turn in (2, 1, 3, 0):
        t = (q + turn) % NQ
        ids = row_ids(t)
        span = pl.ds(pl.multiple_of(t * TILE, TILE), TILE)
        row_part = rrow[span]
        row_part = jnp.concatenate([row_part, row_part], axis=1)
        for j in range(NZ // 2):
            col_part = jnp.concatenate([rcol[2 * j], rcol[2 * j + 1]], axis=1)
            value = ebuf[j, span] * (row_part + col_part)
            value = value - jnp.where(mates(j) == ids, 2.0, 0.0)
            coeff[:, j * TILE : j * TILE + TILE] = value.astype(BF16)
        dz = jnp.dot(coeff[...], keys_all, preferred_element_type=F32)
        psend[pl.ds(t * NX, NX)] = dz.astype(BF16).reshape(NX, HALF, WIDTH)
        if turn == 0:
            prec[mine] = psend[mine]
        loop(max(1, turn * NX), turn * NX + NX, lambda i: dz_copy(i).start())
    pending.append(lambda: loop(1, PLANE, lambda i: dz_copy(i).wait_send()))

    for d, flip in others:
        pos_copy(d, flip).wait_recv()
    pos = smsg[0]
    for n in range(1, 2 * NZ):
        pos = pos + smsg[n]
    loss_ref[...] -= pos

    loop(1, PLANE, lambda i: dz_copy(i).wait_recv())
    acc = prec[0].astype(F32)
    for p in range(1, PLANE):
        acc = acc + prec[p].astype(F32)
    acc = acc * 10.0
    hf = feats[pl.ds(half, HALF)].astype(F32)
    scale = lax.rsqrt(jnp.sum(hf * hf, axis=-1, keepdims=True) + 1e-06)
    unit = hf * scale
    grad_ref[pl.ds(half, HALF)] = scale * (acc - unit * jnp.sum(unit * acc, axis=-1, keepdims=True))
    part = grad_ref.at[pl.ds(half, HALF)]
    last = remote(part, part, fin_s, fin_r, device(0, 0, 0, 1))
    last.start()
    finish()
    last.wait()


def on_device(feats, partner):
    vmem = pl.BlockSpec(memory_space=pltpu.VMEM)
    hbm = pl.BlockSpec(memory_space=pltpu.HBM)
    dma = pltpu.SemaphoreType.DMA
    grad, loss = pl.pallas_call(
        kernel,
        out_shape=(
            jax.ShapeDtypeStruct((ROWS, WIDTH), F32),
            jax.ShapeDtypeStruct((1, ROWS), F32),
        ),
        in_specs=[hbm, hbm],
        out_specs=(vmem, vmem),
        scratch_shapes=[
            pltpu.VMEM((ROWS, WIDTH), BF16),
            pltpu.VMEM((PLANE, HALF, WIDTH), BF16),
            pltpu.VMEM((NZ, ROWS, WIDTH), BF16),
            pltpu.VMEM((NZ, 1, ROWS), jnp.int32),
            pltpu.VMEM((NZ // 2, NR, TILE), F32),
            pltpu.VMEM((NR, ROWS), F32),
            pltpu.VMEM((8, ROWS), F32),
            pltpu.VMEM((PLANE, 8, ROWS), F32),
            pltpu.VMEM((NZ, 1, ROWS), F32),
            pltpu.VMEM((2 * NZ, NZ, 1, ROWS), F32),
            pltpu.VMEM((NZ, 1, ROWS), F32),
            pltpu.VMEM((2 * NZ, 1, ROWS), F32),
            pltpu.VMEM((NZ, 1, ROWS), F32),
            pltpu.VMEM((ROWS, ROWS), F32),
            pltpu.VMEM((NR, ROWS), F32),
            pltpu.VMEM((TILE, NZ * ROWS), BF16),
            pltpu.VMEM((PLANE, HALF, WIDTH), BF16),
            pltpu.VMEM((PLANE, HALF, WIDTH), BF16),
            dma((2,)),
        ]
        + [dma((PLANE,))] * 2
        + [dma((6 * CHUNKS,))] * 2
        + [dma((6,))] * 2
        + [dma((NZ,))] * 2
        + [dma((PLANE,))] * 2
        + [dma((2 * NZ,))] * 6
        + [dma((PLANE,))] * 2
        + [dma] * 2,
        compiler_params=pltpu.CompilerParams(
            collective_id=0, has_side_effects=True
        ),
    )(feats, partner.reshape(1, ROWS))
    return grad, loss.reshape(ROWS)


def solution(mesh):
    in_specs = (P("batch", None), P("batch"))
    out_specs = (P("batch", None), P("batch"))
    return jax.shard_map(
        on_device, mesh=mesh, in_specs=in_specs, out_specs=out_specs, check_vma=False
    )
```

```python
import jax
import jax.numpy as jnp
from jax import lax
from jax.experimental import pallas as pl
from jax.experimental.pallas import tpu as pltpu
from jax.sharding import PartitionSpec as P

MESH = pl.DeviceIdType.MESH
F32 = jnp.float32
BF16 = jnp.bfloat16

NX, NY, NZ = 4, 8, 12
NQ = 4
PLANE = NX * NQ
ROWS, WIDTH = 128, 512
HALF = ROWS // 2
NR = PLANE * HALF
TILE = 256
CHUNKS = 4
CHUNK = ROWS // CHUNKS
NEAR = 9


def kernel(
    feats_hbm,
    partner_hbm,
    grad_ref,
    loss_ref,
    feats,
    rows,
    cols,
    colp,
    ebuf,
    dacc,
    rsend,
    rmsg,
    csend,
    cmsg,
    ssend,
    smsg,
    rcol,
    square,
    rrow,
    coeff,
    psend,
    prec,
    final,
    in_sem,
    row_s,
    row_r,
    ring_s,
    ring_r,
    pair_s,
    pair_r,
    part_s,
    part_r,
    sum_s,
    sum_r,
    near_s,
    near_r,
    far_s,
    far_r,
    pos_s,
    pos_r,
    dz_s,
    dz_r,
    fin_s,
    fin_r,
):
    block = lax.axis_index("batch")
    layer = lax.axis_index("rep")
    x = block % NX
    z = (block // NX) % NZ
    q = block // (NX * NZ)
    core = layer % 2
    y = (layer // 2) * NQ + q
    mine = q * NX + x

    def device(dx, dy, dz, flip):
        ny = (y + dy) % NY
        nz = (z + dz) % NZ
        nx = (x + dx) % NX
        return ((ny % NQ) * (NX * NZ) + nz * NX + nx, (ny // NQ) * 2 + (core + flip) % 2)

    def remote(src, dst, send_sem, recv_sem, target):
        return pltpu.make_async_remote_copy(
            src_ref=src,
            dst_ref=dst,
            send_sem=send_sem,
            recv_sem=recv_sem,
            device_id=target,
            device_id_type=MESH,
        )

    def y_step(dyi):
        return dyi + (dyi // 3) * 4 + (dyi // 2 - dyi // 3) * 4 * core

    def plane_dest(i):
        return device(i % NX, y_step(i // NX), 0, 0)

    def plane_source(i):
        return device(NX - i % NX, NY - y_step(i // NX), 0, 0)

    def plane_dest_slot(i):
        return ((q + i // NX) % NQ) * NX + (x + i % NX) % NX

    def line_dest(i):
        return device(0, 0, i // 2, i % 2)

    fetch = [
        pltpu.make_async_copy(feats_hbm, feats, in_sem.at[0]),
        pltpu.make_async_copy(partner_hbm, colp.at[0], in_sem.at[1]),
    ]
    for copy in fetch:
        copy.start()

    barrier = pltpu.get_barrier_semaphore()

    def greet_plane(i, carry):
        pl.semaphore_signal(barrier, inc=1, device_id=plane_source(i), device_id_type=MESH)
        return carry

    ahead = 1 + (NZ - 2) * core
    for dz, flip in ((NZ - ahead, 0), (ahead, 1), (0, 1)):
        pl.semaphore_signal(
            barrier, inc=1, device_id=device(0, 0, dz, flip), device_id_type=MESH
        )
    lax.fori_loop(1, PLANE, greet_plane, 0)
    for copy in fetch:
        copy.wait()

    hf = feats[...].astype(F32)
    scale = lax.rsqrt(jnp.sum(hf * hf, axis=-1, keepdims=True) + 1e-06)
    embed = (hf * scale).astype(BF16)
    cols[0] = embed
    half = pl.multiple_of(core * HALF, HALF)
    rows[mine] = cols[0, pl.ds(half, HALF), :]

    pl.semaphore_wait(barrier, PLANE - 1 + 3)

    LAST = NZ // 2

    def ring_slot(k):
        if k == 0:
            return 0
        return 1 if k == LAST else 2 * k + 1 - core

    def chunk_rows(h):
        return pl.ds(pl.multiple_of((2 * core + h) % CHUNKS * CHUNK, CHUNK), CHUNK)

    def ring_copy(k, h):
        n = (k - 1) * CHUNKS + h
        target = device(0, 0, ahead, 0)
        if k == LAST:
            target = device(0, 0, ahead, h // 2)
            h = h % 2
        return remote(
            cols.at[ring_slot(k - 1), chunk_rows(h)],
            cols.at[ring_slot(k), chunk_rows(h)],
            ring_s.at[n],
            ring_r.at[n],
            target,
        )

    def pair_copy(k):
        part = cols.at[ring_slot(k)]
        return remote(part, part, pair_s.at[k - 1], pair_r.at[k - 1], device(0, 0, 0, 1))

    def mate_copy(k):
        return remote(
            colp.at[ring_slot(k - 1)],
            colp.at[ring_slot(k)],
            part_s.at[k - 1],
            part_r.at[k - 1],
            device(0, 0, ahead, 0),
        )

    def mate_pair_copy(k):
        part = colp.at[ring_slot(k)]
        return remote(part, part, part_s.at[5 + k], part_r.at[5 + k], device(0, 0, 0, 1))

    def row_copy(i):
        return remote(
            cols.at[0, pl.ds(half, HALF)], rows.at[mine], row_s.at[i], row_r.at[i], plane_dest(i)
        )

    def slot_of(off):
        off = off % NZ
        if off in (0, LAST):
            return off // LAST
        return 2 * off if off < LAST else 2 * (NZ - off) + 1

    def loop(lo, hi, act):
        def body(i, carry):
            act(i)
            return carry

        lax.fori_loop(lo, hi, body, 0)

    pending = []

    def finish():
        for settle in pending:
            settle()

    for h in range(CHUNKS):
        ring_copy(1, h).start()
    mate_copy(1).start()
    for dyi in (0, 1, 3, 2):
        loop(max(1, dyi * NX), dyi * NX + NX, lambda i: row_copy(i).start())

    def settle_gather():
        for k in range(1, LAST + 1):
            for h in range(CHUNKS):
                ring_copy(k, h).wait_send()
            mate_copy(k).wait_send()
            if k < LAST:
                pair_copy(k).wait_send()
                mate_pair_copy(k).wait_send()
        loop(1, PLANE, lambda i: row_copy(i).wait_send())

    pending.append(settle_gather)

    def ring_step(k):
        for h in range(CHUNKS):
            ring_copy(k, h).wait_recv()
            if k < LAST - 1:
                ring_copy(k + 1, h).start()
            elif k == LAST - 1 and h < CHUNKS // 2:
                ring_copy(k + 1, h).start()
                ring_copy(k + 1, h + 2).start()
        mate_copy(k).wait_recv()
        if k < LAST:
            mate_copy(k + 1).start()
            pair_copy(k).start()
            mate_pair_copy(k).start()

    def pair_in(k):
        pair_copy(k).wait_recv()
        mate_pair_copy(k).wait_recv()

    def rows_in(turn):
        dyi = (NQ - turn) % NQ
        loop(max(1, dyi * NX), dyi * NX + NX, lambda i: row_copy(i).wait_recv())

    lane = lax.broadcasted_iota(jnp.int32, (1, ROWS), 1)
    row_in_tile = lax.broadcasted_iota(jnp.int32, (TILE, 1), 0)

    def row_ids(t):
        return (t * NZ * NX + z * NX) * ROWS + core * HALF + (row_in_tile // HALF) * HALF + row_in_tile

    def mates(j):
        return jnp.concatenate([colp[2 * j], colp[2 * j + 1]], axis=1)

    def score_of(t, keys):
        return lax.dot_general(
            rows[pl.ds(t * NX, NX)].reshape(TILE, WIDTH),
            keys,
            (((1,), (1,)), ((), ())),
            preferred_element_type=F32,
        ) * 10.0

    def place(slot):
        return slot - 1 if slot > 1 else slot * (NZ - 1)

    def sums(turn, slot, weight, hits):
        weight = jnp.sum(weight, axis=0, keepdims=True)
        hits = jnp.sum(hits, axis=0, keepdims=True)
        if turn == 0:
            csend[place(slot)] = weight
            ssend[place(slot)] = hits
        else:
            csend[place(slot)] += weight
            ssend[place(slot)] += hits

    def single(turn, slot):
        t = (q + turn) % NQ
        ids = row_ids(t)
        span = pl.ds(pl.multiple_of(t * TILE, TILE), TILE)
        score = score_of(t, cols[slot])
        weight = jnp.exp(score - 10.0)
        if slot == 0 and turn == 0:
            key_ids = block * ROWS + lane
            weight = jnp.where(key_ids == ids, 0.0, weight)
        hits = jnp.where(colp[slot] == ids, score, 0.0)
        ebuf[0, span, slot * ROWS : slot * ROWS + ROWS] = weight
        if slot == 0:
            dacc[span] = weight
        else:
            dacc[span] += weight
        sums(turn, slot, weight, hits)

    def pair(turn, j):
        t = (q + turn) % NQ
        ids = row_ids(t)
        span = pl.ds(pl.multiple_of(t * TILE, TILE), TILE)
        score = score_of(t, cols[2 * j : 2 * j + 2].reshape(TILE, WIDTH))
        weight = jnp.exp(score - 10.0)
        hits = jnp.where(mates(j) == ids, score, 0.0)
        ebuf[j, span] = weight
        dacc[span] += weight[:, :ROWS] + weight[:, ROWS:]
        for side in range(2):
            cut = slice(side * ROWS, side * ROWS + ROWS)
            sums(turn, 2 * j + side, weight[:, cut], hits[:, cut])

    def near_copy(i):
        return remote(
            csend.at[pl.ds(0, NEAR)],
            cmsg.at[i // 2 * 2 + core, pl.ds(0, NEAR)],
            near_s.at[i],
            near_r.at[i],
            line_dest(i),
        )

    def far_copy(i):
        return remote(
            csend.at[pl.ds(NEAR, NZ - NEAR)],
            cmsg.at[i // 2 * 2 + core, pl.ds(NEAR, NZ - NEAR)],
            far_s.at[i],
            far_r.at[i],
            line_dest(i),
        )

    ring_step(1)
    ring_step(2)
    ring_step(3)
    rows_in(0)
    single(0, 0)
    pair_in(1)
    pair(0, 1)
    pair_in(2)
    pair(0, 2)
    ring_step(4)
    rows_in(3)
    rows_in(1)
    for turn in (1, 3):
        single(turn, 0)
        pair(turn, 1)
    pair_in(3)
    pair(0, 3)
    ring_step(5)
    for turn in (1, 3):
        pair(turn, 2)
        pair(turn, 3)
    pair_in(4)
    for turn in (0, 1, 3):
        pair(turn, 4)
    rows_in(2)
    single(2, 0)
    for j in range(1, 5):
        pair(2, j)
    pair_in(5)
    loop(1, NZ, lambda i: near_copy(i).start())
    loop(NZ + 2, 2 * NZ, lambda i: near_copy(i).start())
    pending.append(lambda: loop(1, 2 * NZ, lambda i: near_copy(i).wait_send()))
    for turn in range(NQ):
        pair(turn, 5)
    ring_step(6)
    loop(NZ, NZ + 2, lambda i: near_copy(i).start())
    for turn in range(NQ):
        single(turn, 1)

    loop(1, 2 * NZ, lambda i: far_copy(i).start())
    pending.append(lambda: loop(1, 2 * NZ, lambda i: far_copy(i).wait_send()))

    for g in range(8):
        span = pl.ds(g * ROWS, ROWS)
        rsend[pl.ds(g, 1)] = jnp.sum(dacc[span].T, axis=0, keepdims=True)

    def sum_copy(i):
        return remote(rsend, rmsg.at[mine], sum_s.at[i], sum_r.at[i], plane_dest(i))

    loop(1, PLANE, lambda i: sum_copy(i).start())
    pending.append(lambda: loop(1, PLANE, lambda i: sum_copy(i).wait_send()))

    def pos_copy(d, flip):
        n = 2 * d + flip
        return remote(
            ssend.at[place(slot_of(d))],
            smsg.at[2 * d + core],
            pos_s.at[n],
            pos_r.at[n],
            device(0, 0, d, flip),
        )

    others = [(d, flip) for d in range(NZ) for flip in range(2) if d + flip]
    for d, flip in others:
        pos_copy(d, flip).start()
    pending.append(lambda: [pos_copy(d, flip).wait_send() for d, flip in others])

    rmsg[mine] = rsend[...]
    cmsg[core] = csend[...]
    smsg[core] = ssend[0]
    loop(1, PLANE, lambda i: sum_copy(i).wait_recv())
    total = rmsg[0]
    for p in range(1, PLANE):
        total = total + rmsg[p]
    square[pl.ds(0, 8)] = 1.0 / total
    turned = square[...].T
    for g in range(8):
        rrow[pl.ds(g * ROWS, ROWS)] = jnp.broadcast_to(turned[:, g : g + 1], (ROWS, ROWS))

    loop(1, 2 * NZ, lambda i: near_copy(i).wait_recv())
    loop(1, 2 * NZ, lambda i: far_copy(i).wait_recv())
    own_den = None
    for off in range(NZ):
        den = None
        for d in range(NZ):
            for c in range(2):
                part = cmsg[2 * d + c, place(slot_of(off + d))]
                den = part if den is None else den + part
        rcol[slot_of(off)] = 1.0 / den
        if off == 0:
            own_den = den
    loss_ref[...] = jnp.log(own_den) + 10.0

    def dz_copy(i):
        return remote(
            psend.at[plane_dest_slot(i)], prec.at[mine], dz_s.at[i], dz_r.at[i], plane_dest(i)
        )

    keys_all = cols[...].reshape(NZ * ROWS, WIDTH)
    for turn in (2, 1, 3, 0):
        t = (q + turn) % NQ
        ids = row_ids(t)
        span = pl.ds(pl.multiple_of(t * TILE, TILE), TILE)
        row_part = rrow[span]
        row_part = jnp.concatenate([row_part, row_part], axis=1)
        for j in range(NZ // 2):
            col_part = jnp.concatenate([rcol[2 * j], rcol[2 * j + 1]], axis=1)
            value = ebuf[j, span] * (row_part + col_part)
            value = value - jnp.where(mates(j) == ids, 2.0, 0.0)
            coeff[:, j * TILE : j * TILE + TILE] = value.astype(BF16)
        dz = jnp.dot(coeff[...], keys_all, preferred_element_type=F32)
        psend[pl.ds(t * NX, NX)] = dz.astype(BF16).reshape(NX, HALF, WIDTH)
        if turn == 0:
            prec[mine] = psend[mine]
        for dx in (2, 1, 3, 0):
            if turn + dx:
                dz_copy(turn * NX + dx).start()
    pending.append(lambda: loop(1, PLANE, lambda i: dz_copy(i).wait_send()))

    for d, flip in others:
        pos_copy(d, flip).wait_recv()
    pos = smsg[0]
    for n in range(1, 2 * NZ):
        pos = pos + smsg[n]
    loss_ref[...] -= pos

    loop(1, PLANE, lambda i: dz_copy(i).wait_recv())
    acc = prec[0].astype(F32)
    for p in range(1, PLANE):
        acc = acc + prec[p].astype(F32)
    acc = acc * 10.0
    hf = feats[pl.ds(half, HALF)].astype(F32)
    scale = lax.rsqrt(jnp.sum(hf * hf, axis=-1, keepdims=True) + 1e-06)
    unit = hf * scale
    final[...] = scale * (acc - unit * jnp.sum(unit * acc, axis=-1, keepdims=True))
    part = grad_ref.at[pl.ds(half, HALF)]
    last = remote(final, part, fin_s, fin_r, device(0, 0, 0, 1))
    last.start()
    keep = pltpu.make_async_copy(final, part, in_sem.at[0])
    keep.start()
    finish()
    keep.wait()
    last.wait()


def on_device(feats, partner):
    vmem = pl.BlockSpec(memory_space=pltpu.VMEM)
    hbm = pl.BlockSpec(memory_space=pltpu.HBM)
    dma = pltpu.SemaphoreType.DMA
    grad, loss = pl.pallas_call(
        kernel,
        out_shape=(
            jax.ShapeDtypeStruct((ROWS, WIDTH), F32),
            jax.ShapeDtypeStruct((1, ROWS), F32),
        ),
        in_specs=[hbm, hbm],
        out_specs=(hbm, vmem),
        scratch_shapes=[
            pltpu.VMEM((ROWS, WIDTH), BF16),
            pltpu.VMEM((PLANE, HALF, WIDTH), BF16),
            pltpu.VMEM((NZ, ROWS, WIDTH), BF16),
            pltpu.VMEM((NZ, 1, ROWS), jnp.int32),
            pltpu.VMEM((NZ // 2, NR, TILE), F32),
            pltpu.VMEM((NR, ROWS), F32),
            pltpu.VMEM((8, ROWS), F32),
            pltpu.VMEM((PLANE, 8, ROWS), F32),
            pltpu.VMEM((NZ, 1, ROWS), F32),
            pltpu.VMEM((2 * NZ, NZ, 1, ROWS), F32),
            pltpu.VMEM((NZ, 1, ROWS), F32),
            pltpu.VMEM((2 * NZ, 1, ROWS), F32),
            pltpu.VMEM((NZ, 1, ROWS), F32),
            pltpu.VMEM((ROWS, ROWS), F32),
            pltpu.VMEM((NR, ROWS), F32),
            pltpu.VMEM((TILE, NZ * ROWS), BF16),
            pltpu.VMEM((PLANE, HALF, WIDTH), BF16),
            pltpu.VMEM((PLANE, HALF, WIDTH), BF16),
            pltpu.VMEM((HALF, WIDTH), F32),
            dma((2,)),
        ]
        + [dma((PLANE,))] * 2
        + [dma((6 * CHUNKS,))] * 2
        + [dma((6,))] * 2
        + [dma((NZ,))] * 2
        + [dma((PLANE,))] * 2
        + [dma((2 * NZ,))] * 6
        + [dma((PLANE,))] * 2
        + [dma] * 2,
        compiler_params=pltpu.CompilerParams(
            collective_id=0, has_side_effects=True
        ),
    )(feats, partner.reshape(1, ROWS))
    return grad, loss.reshape(ROWS)


def solution(mesh):
    in_specs = (P("batch", None), P("batch"))
    out_specs = (P("batch", None), P("batch"))
    return jax.shard_map(
        on_device, mesh=mesh, in_specs=in_specs, out_specs=out_specs, check_vma=False
    )
```

```python
import jax
import jax.numpy as jnp
from jax import lax
from jax.experimental import pallas as pl
from jax.experimental.pallas import tpu as pltpu
from jax.sharding import PartitionSpec as P

MESH = pl.DeviceIdType.MESH
F32 = jnp.float32
BF16 = jnp.bfloat16

NX, NY, NZ = 4, 8, 12
NQ = 4
PLANE = NX * NQ
ROWS, WIDTH = 128, 512
HALF = ROWS // 2
NR = PLANE * HALF
TILE = 256
CHUNKS = 4
CHUNK = ROWS // CHUNKS
FAR_FIRST = [2 * d + f for d in (6, 5, 7, 4, 8, 3, 9, 2, 10, 1, 11) for f in (0, 1)] + [1]
NEAR = 9


def kernel(
    feats_hbm,
    partner_hbm,
    grad_ref,
    loss_ref,
    feats,
    rows,
    cols,
    colp,
    ebuf,
    dacc,
    rsend,
    rmsg,
    csend,
    cmsg,
    ssend,
    smsg,
    rcol,
    square,
    rrow,
    coeff,
    psend,
    prec,
    final,
    in_sem,
    row_s,
    row_r,
    ring_s,
    ring_r,
    pair_s,
    pair_r,
    part_s,
    part_r,
    sum_s,
    sum_r,
    near_s,
    near_r,
    far_s,
    far_r,
    pos_s,
    pos_r,
    dz_s,
    dz_r,
    fin_s,
    fin_r,
):
    block = lax.axis_index("batch")
    layer = lax.axis_index("rep")
    x = lax.rem(block, NX)
    z = lax.rem(lax.div(block, NX), NZ)
    q = lax.div(block, NX * NZ)
    core = lax.rem(layer, 2)
    y = lax.div(layer, 2) * NQ + q
    mine = q * NX + x

    def device(dx, dy, dz, flip):
        return (plane_base(dx, dy) + line_base(dz), layer_base(dy) + side(flip))

    def still(step):
        return isinstance(step, int) and step == 0

    def plane_base(dx, dy):
        nx = x if still(dx) else lax.rem(x + dx, NX)
        ny = q if still(dy) else lax.rem(q + dy, NQ)
        return ny * (NX * NZ) + nx

    def line_base(dz):
        return (z if still(dz) else lax.rem(z + dz, NZ)) * NX

    def layer_base(dy):
        return layer - core if still(dy) else lax.div(lax.rem(y + dy, NY), NQ) * 2

    def side(flip):
        return core if still(flip) else 1 - core

    def remote(src, dst, send_sem, recv_sem, target):
        return pltpu.make_async_remote_copy(
            src_ref=src,
            dst_ref=dst,
            send_sem=send_sem,
            recv_sem=recv_sem,
            device_id=target,
            device_id_type=MESH,
        )

    def y_step(dyi):
        if isinstance(dyi, int):
            return (0, 1, 2 + 4 * core, 7)[dyi]
        return dyi + (dyi // 3) * 4 + (dyi // 2 - dyi // 3) * 4 * core

    def plane_dest(i):
        return device(i % NX, y_step(i // NX), 0, 0)

    def plane_source(i):
        dx, dyi = i % NX, i // NX
        return device((NX - dx) % NX, (0, 7, 6 - 4 * core, 1)[dyi], 0, 0)

    def plane_dest_slot(i):
        return lax.rem(q + i // NX, NQ) * NX + lax.rem(x + i % NX, NX)

    def line_dest(i):
        return device(0, 0, i // 2, i % 2)

    fetch = [
        pltpu.make_async_copy(feats_hbm, feats, in_sem.at[0]),
        pltpu.make_async_copy(partner_hbm, colp.at[0], in_sem.at[1]),
    ]
    for copy in fetch:
        copy.start()

    barrier = pltpu.get_barrier_semaphore()

    ahead = 1 + (NZ - 2) * core
    for dz, flip in ((NZ - ahead, 0), (ahead, 1), (0, 1)):
        pl.semaphore_signal(
            barrier, inc=1, device_id=device(0, 0, dz, flip), device_id_type=MESH
        )
    for i in range(1, PLANE):
        pl.semaphore_signal(barrier, inc=1, device_id=plane_source(i), device_id_type=MESH)
    for copy in fetch:
        copy.wait()

    hf = feats[...].astype(F32)
    scale = lax.rsqrt(jnp.sum(hf * hf, axis=-1, keepdims=True) + 1e-06)
    embed = (hf * scale).astype(BF16)
    cols[0] = embed
    half = pl.multiple_of(core * HALF, HALF)
    rows[mine] = cols[0, pl.ds(half, HALF), :]

    pl.semaphore_wait(barrier, PLANE - 1 + 3)

    LAST = NZ // 2

    def ring_slot(k):
        if k == 0:
            return 0
        return 1 if k == LAST else 2 * k + 1 - core

    def chunk_rows(h):
        return pl.ds(pl.multiple_of((2 * core + h) % CHUNKS * CHUNK, CHUNK), CHUNK)

    def ring_copy(k, h):
        n = (k - 1) * CHUNKS + h
        target = device(0, 0, ahead, 0)
        if k == LAST:
            target = device(0, 0, ahead, h // 2)
            h = h % 2
        return remote(
            cols.at[ring_slot(k - 1), chunk_rows(h)],
            cols.at[ring_slot(k), chunk_rows(h)],
            ring_s.at[n],
            ring_r.at[n],
            target,
        )

    def pair_copy(k):
        part = cols.at[ring_slot(k)]
        return remote(part, part, pair_s.at[k - 1], pair_r.at[k - 1], device(0, 0, 0, 1))

    def mate_copy(k):
        return remote(
            colp.at[ring_slot(k - 1)],
            colp.at[ring_slot(k)],
            part_s.at[k - 1],
            part_r.at[k - 1],
            device(0, 0, ahead, 0),
        )

    def mate_pair_copy(k):
        part = colp.at[ring_slot(k)]
        return remote(part, part, part_s.at[5 + k], part_r.at[5 + k], device(0, 0, 0, 1))

    def row_copy(i):
        return remote(
            cols.at[0, pl.ds(half, HALF)], rows.at[mine], row_s.at[i], row_r.at[i], plane_dest(i)
        )

    def slot_of(off):
        off = off % NZ
        if off in (0, LAST):
            return off // LAST
        return 2 * off if off < LAST else 2 * (NZ - off) + 1

    def loop(lo, hi, act):
        def body(i, carry):
            act(i)
            return carry

        lax.fori_loop(lo, hi, body, 0)

    pending = []

    def finish():
        for settle in pending:
            settle()

    for h in range(CHUNKS):
        ring_copy(1, h).start()
    mate_copy(1).start()
    for dyi in (0, 1, 3, 2):
        for i in range(max(1, dyi * NX), dyi * NX + NX):
            row_copy(i).start()

    def settle_gather():
        for k in range(1, LAST + 1):
            for h in range(CHUNKS):
                ring_copy(k, h).wait_send()
            mate_copy(k).wait_send()
            if k < LAST:
                pair_copy(k).wait_send()
                mate_pair_copy(k).wait_send()
        loop(1, PLANE, lambda i: row_copy(i).wait_send())

    pending.append(settle_gather)

    def ring_step(k):
        for h in range(CHUNKS):
            ring_copy(k, h).wait_recv()
            if k < LAST - 1:
                ring_copy(k + 1, h).start()
            elif k == LAST - 1 and h < CHUNKS // 2:
                ring_copy(k + 1, h).start()
                ring_copy(k + 1, h + 2).start()
        mate_copy(k).wait_recv()
        if k < LAST:
            mate_copy(k + 1).start()
            pair_copy(k).start()
            mate_pair_copy(k).start()

    def pair_in(k):
        pair_copy(k).wait_recv()
        mate_pair_copy(k).wait_recv()

    def rows_in(turn):
        dyi = (NQ - turn) % NQ
        loop(max(1, dyi * NX), dyi * NX + NX, lambda i: row_copy(i).wait_recv())

    lane = lax.broadcasted_iota(jnp.int32, (1, ROWS), 1)
    row_in_tile = lax.broadcasted_iota(jnp.int32, (TILE, 1), 0)

    def row_ids(t):
        return (t * NZ * NX + z * NX) * ROWS + core * HALF + (row_in_tile // HALF) * HALF + row_in_tile

    def mates(j):
        return jnp.concatenate([colp[2 * j], colp[2 * j + 1]], axis=1)

    def score_of(t, keys):
        return lax.dot_general(
            rows[pl.ds(t * NX, NX)].reshape(TILE, WIDTH),
            keys,
            (((1,), (1,)), ((), ())),
            preferred_element_type=F32,
        ) * 10.0

    def place(slot):
        return slot - 1 if slot > 1 else slot * (NZ - 1)

    def sums(turn, slot, weight, hits):
        weight = jnp.sum(weight, axis=0, keepdims=True)
        hits = jnp.sum(hits, axis=0, keepdims=True)
        if turn == 0:
            csend[place(slot)] = weight
            ssend[place(slot)] = hits
        else:
            csend[place(slot)] += weight
            ssend[place(slot)] += hits

    def single(turn, slot):
        t = (q + turn) % NQ
        ids = row_ids(t)
        span = pl.ds(pl.multiple_of(t * TILE, TILE), TILE)
        score = score_of(t, cols[slot])
        weight = jnp.exp(score - 10.0)
        if slot == 0 and turn == 0:
            key_ids = block * ROWS + lane
            weight = jnp.where(key_ids == ids, 0.0, weight)
        hits = jnp.where(colp[slot] == ids, score, 0.0)
        ebuf[0, span, slot * ROWS : slot * ROWS + ROWS] = weight
        if slot == 0:
            dacc[span] = weight
        else:
            dacc[span] += weight
        sums(turn, slot, weight, hits)

    def pair(turn, j):
        t = (q + turn) % NQ
        ids = row_ids(t)
        span = pl.ds(pl.multiple_of(t * TILE, TILE), TILE)
        score = score_of(t, cols[2 * j : 2 * j + 2].reshape(TILE, WIDTH))
        weight = jnp.exp(score - 10.0)
        hits = jnp.where(mates(j) == ids, score, 0.0)
        ebuf[j, span] = weight
        dacc[span] += weight[:, :ROWS] + weight[:, ROWS:]
        for side in range(2):
            cut = slice(side * ROWS, side * ROWS + ROWS)
            sums(turn, 2 * j + side, weight[:, cut], hits[:, cut])

    def near_copy(i):
        return remote(
            csend.at[pl.ds(0, NEAR)],
            cmsg.at[i // 2 * 2 + core, pl.ds(0, NEAR)],
            near_s.at[i],
            near_r.at[i],
            line_dest(i),
        )

    def far_copy(i):
        return remote(
            csend.at[pl.ds(NEAR, NZ - NEAR)],
            cmsg.at[i // 2 * 2 + core, pl.ds(NEAR, NZ - NEAR)],
            far_s.at[i],
            far_r.at[i],
            line_dest(i),
        )

    ring_step(1)
    ring_step(2)
    ring_step(3)
    rows_in(0)
    single(0, 0)
    pair_in(1)
    pair(0, 1)
    pair_in(2)
    pair(0, 2)
    ring_step(4)
    rows_in(3)
    rows_in(1)
    for turn in (1, 3):
        single(turn, 0)
        pair(turn, 1)
    pair_in(3)
    pair(0, 3)
    ring_step(5)
    for turn in (1, 3):
        pair(turn, 2)
        pair(turn, 3)
    pair_in(4)
    for turn in (0, 1, 3):
        pair(turn, 4)
    rows_in(2)
    single(2, 0)
    for j in range(1, 5):
        pair(2, j)
    pair_in(5)
    for i in FAR_FIRST[2:]:
        near_copy(i).start()
    pending.append(lambda: loop(1, 2 * NZ, lambda i: near_copy(i).wait_send()))
    for turn in range(NQ):
        pair(turn, 5)
    ring_step(6)
    for i in FAR_FIRST[:2]:
        near_copy(i).start()
    for turn in range(NQ):
        single(turn, 1)

    for i in FAR_FIRST:
        far_copy(i).start()
    pending.append(lambda: loop(1, 2 * NZ, lambda i: far_copy(i).wait_send()))

    for g in range(8):
        span = pl.ds(g * ROWS, ROWS)
        rsend[pl.ds(g, 1)] = jnp.sum(dacc[span].T, axis=0, keepdims=True)

    def sum_copy(i):
        return remote(rsend, rmsg.at[mine], sum_s.at[i], sum_r.at[i], plane_dest(i))

    for dyi in (2, 1, 3, 0):
        for dx in (2, 1, 3, 0):
            if dyi + dx:
                sum_copy(dyi * NX + dx).start()
    pending.append(lambda: loop(1, PLANE, lambda i: sum_copy(i).wait_send()))

    def pos_copy(d, flip):
        n = 2 * d + flip
        return remote(
            ssend.at[place(slot_of(d))],
            smsg.at[2 * d + core],
            pos_s.at[n],
            pos_r.at[n],
            device(0, 0, d, flip),
        )

    others = [(d, flip) for d in range(NZ) for flip in range(2) if d + flip]

    rmsg[mine] = rsend[...]
    cmsg[core] = csend[...]
    smsg[core] = ssend[0]
    loop(1, PLANE, lambda i: sum_copy(i).wait_recv())
    total = rmsg[0]
    for p in range(1, PLANE):
        total = total + rmsg[p]
    square[pl.ds(0, 8)] = 1.0 / total
    turned = square[...].T
    for g in range(8):
        rrow[pl.ds(g * ROWS, ROWS)] = jnp.broadcast_to(turned[:, g : g + 1], (ROWS, ROWS))

    loop(1, 2 * NZ, lambda i: near_copy(i).wait_recv())
    loop(1, 2 * NZ, lambda i: far_copy(i).wait_recv())
    own_den = None
    for off in range(NZ):
        den = None
        for d in range(NZ):
            for c in range(2):
                part = cmsg[2 * d + c, place(slot_of(off + d))]
                den = part if den is None else den + part
        rcol[slot_of(off)] = 1.0 / den
        if off == 0:
            own_den = den
    loss_ref[...] = jnp.log(own_den) + 10.0

    def dz_copy(i):
        return remote(
            psend.at[plane_dest_slot(i)], prec.at[mine], dz_s.at[i], dz_r.at[i], plane_dest(i)
        )

    keys_all = cols[...].reshape(NZ * ROWS, WIDTH)
    for turn in (2, 1, 3, 0):
        t = (q + turn) % NQ
        ids = row_ids(t)
        span = pl.ds(pl.multiple_of(t * TILE, TILE), TILE)
        row_part = rrow[span]
        row_part = jnp.concatenate([row_part, row_part], axis=1)
        for j in range(NZ // 2):
            col_part = jnp.concatenate([rcol[2 * j], rcol[2 * j + 1]], axis=1)
            value = ebuf[j, span] * (row_part + col_part)
            value = value - jnp.where(mates(j) == ids, 2.0, 0.0)
            coeff[:, j * TILE : j * TILE + TILE] = value.astype(BF16)
        dz = jnp.dot(coeff[...], keys_all, preferred_element_type=F32)
        psend[pl.ds(t * NX, NX)] = dz.astype(BF16).reshape(NX, HALF, WIDTH)
        if turn == 0:
            prec[mine] = psend[mine]
        for dx in (2, 1, 3, 0):
            if turn + dx:
                dz_copy(turn * NX + dx).start()
    pending.append(lambda: loop(1, PLANE, lambda i: dz_copy(i).wait_send()))

    for d, flip in others:
        pos_copy(d, flip).start()
    pending.append(lambda: [pos_copy(d, flip).wait_send() for d, flip in others])
    for d, flip in others:
        pos_copy(d, flip).wait_recv()
    pos = smsg[0]
    for n in range(1, 2 * NZ):
        pos = pos + smsg[n]
    loss_ref[...] -= pos

    loop(1, PLANE, lambda i: dz_copy(i).wait_recv())
    acc = prec[0].astype(F32)
    for p in range(1, PLANE):
        acc = acc + prec[p].astype(F32)
    acc = acc * 10.0
    hf = feats[pl.ds(half, HALF)].astype(F32)
    scale = lax.rsqrt(jnp.sum(hf * hf, axis=-1, keepdims=True) + 1e-06)
    unit = hf * scale
    final[...] = scale * (acc - unit * jnp.sum(unit * acc, axis=-1, keepdims=True))
    part = grad_ref.at[pl.ds(half, HALF)]
    last = remote(final, part, fin_s, fin_r, device(0, 0, 0, 1))
    last.start()
    keep = pltpu.make_async_copy(final, part, in_sem.at[0])
    keep.start()
    finish()
    keep.wait()
    last.wait()


def on_device(feats, partner):
    vmem = pl.BlockSpec(memory_space=pltpu.VMEM)
    hbm = pl.BlockSpec(memory_space=pltpu.HBM)
    dma = pltpu.SemaphoreType.DMA
    grad, loss = pl.pallas_call(
        kernel,
        out_shape=(
            jax.ShapeDtypeStruct((ROWS, WIDTH), F32),
            jax.ShapeDtypeStruct((1, ROWS), F32),
        ),
        in_specs=[hbm, hbm],
        out_specs=(hbm, vmem),
        scratch_shapes=[
            pltpu.VMEM((ROWS, WIDTH), BF16),
            pltpu.VMEM((PLANE, HALF, WIDTH), BF16),
            pltpu.VMEM((NZ, ROWS, WIDTH), BF16),
            pltpu.VMEM((NZ, 1, ROWS), jnp.int32),
            pltpu.VMEM((NZ // 2, NR, TILE), F32),
            pltpu.VMEM((NR, ROWS), F32),
            pltpu.VMEM((8, ROWS), F32),
            pltpu.VMEM((PLANE, 8, ROWS), F32),
            pltpu.VMEM((NZ, 1, ROWS), F32),
            pltpu.VMEM((2 * NZ, NZ, 1, ROWS), F32),
            pltpu.VMEM((NZ, 1, ROWS), F32),
            pltpu.VMEM((2 * NZ, 1, ROWS), F32),
            pltpu.VMEM((NZ, 1, ROWS), F32),
            pltpu.VMEM((ROWS, ROWS), F32),
            pltpu.VMEM((NR, ROWS), F32),
            pltpu.VMEM((TILE, NZ * ROWS), BF16),
            pltpu.VMEM((PLANE, HALF, WIDTH), BF16),
            pltpu.VMEM((PLANE, HALF, WIDTH), BF16),
            pltpu.VMEM((HALF, WIDTH), F32),
            dma((2,)),
        ]
        + [dma((PLANE,))] * 2
        + [dma((6 * CHUNKS,))] * 2
        + [dma((6,))] * 2
        + [dma((NZ,))] * 2
        + [dma((PLANE,))] * 2
        + [dma((2 * NZ,))] * 6
        + [dma((PLANE,))] * 2
        + [dma] * 2,
        compiler_params=pltpu.CompilerParams(
            collective_id=0, has_side_effects=True
        ),
    )(feats, partner.reshape(1, ROWS))
    return grad, loss.reshape(ROWS)


def solution(mesh):
    in_specs = (P("batch", None), P("batch"))
    out_specs = (P("batch", None), P("batch"))
    return jax.shard_map(
        on_device, mesh=mesh, in_specs=in_specs, out_specs=out_specs, check_vma=False
    )
```

```python
import jax
import jax.numpy as jnp
from jax import lax
from jax.experimental import pallas as pl
from jax.experimental.pallas import tpu as pltpu
from jax.sharding import PartitionSpec as P

MESH = pl.DeviceIdType.MESH
F32 = jnp.float32
BF16 = jnp.bfloat16

NX, NY, NZ = 4, 8, 12
NQ = 4
PLANE = NX * NQ
ROWS, WIDTH = 128, 512
HALF = ROWS // 2
NR = PLANE * HALF
TILE = 256
CHUNKS = 4
CHUNK = ROWS // CHUNKS
FAR_FIRST = [2 * d + f for d in (6, 5, 7, 4, 8, 3, 9, 2, 10, 1, 11) for f in (0, 1)] + [1]
NEAR = 9


def kernel(
    feats_hbm,
    partner_hbm,
    grad_ref,
    loss_ref,
    feats,
    rows,
    cols,
    colp,
    ebuf,
    dacc,
    rsend,
    rmsg,
    csend,
    cmsg,
    ssend,
    smsg,
    rcol,
    square,
    rrow,
    coeff,
    psend,
    prec,
    final,
    in_sem,
    row_s,
    row_r,
    ring_s,
    ring_r,
    pair_s,
    pair_r,
    part_s,
    part_r,
    sum_s,
    sum_r,
    near_s,
    near_r,
    far_s,
    far_r,
    pos_s,
    pos_r,
    dz_s,
    dz_r,
    fin_s,
    fin_r,
):
    block = lax.axis_index("batch")
    layer = lax.axis_index("rep")
    x = lax.rem(block, NX)
    z = lax.rem(lax.div(block, NX), NZ)
    q = lax.div(block, NX * NZ)
    core = lax.rem(layer, 2)
    y = lax.div(layer, 2) * NQ + q
    mine = q * NX + x

    def device(dx, dy, dz, flip):
        return (plane_base(dx, dy) + line_base(dz), layer_base(dy) + side(flip))

    def still(step):
        return isinstance(step, int) and step == 0

    def plane_base(dx, dy):
        nx = x if still(dx) else lax.rem(x + dx, NX)
        ny = q if still(dy) else lax.rem(q + dy, NQ)
        return ny * (NX * NZ) + nx

    def line_base(dz):
        return (z if still(dz) else lax.rem(z + dz, NZ)) * NX

    def layer_base(dy):
        return layer - core if still(dy) else lax.div(lax.rem(y + dy, NY), NQ) * 2

    def side(flip):
        return core if still(flip) else 1 - core

    def remote(src, dst, send_sem, recv_sem, target):
        return pltpu.make_async_remote_copy(
            src_ref=src,
            dst_ref=dst,
            send_sem=send_sem,
            recv_sem=recv_sem,
            device_id=target,
            device_id_type=MESH,
        )

    def y_step(dyi):
        if isinstance(dyi, int):
            return (0, 1, 2 + 4 * core, 7)[dyi]
        return dyi + (dyi // 3) * 4 + (dyi // 2 - dyi // 3) * 4 * core

    def plane_dest(i):
        return device(i % NX, y_step(i // NX), 0, 0)

    def plane_source(i):
        dx, dyi = i % NX, i // NX
        return device((NX - dx) % NX, (0, 7, 6 - 4 * core, 1)[dyi], 0, 0)

    def plane_dest_slot(i):
        return lax.rem(q + i // NX, NQ) * NX + lax.rem(x + i % NX, NX)

    def line_dest(i):
        return device(0, 0, i // 2, i % 2)

    fetch = [
        pltpu.make_async_copy(feats_hbm, feats, in_sem.at[0]),
        pltpu.make_async_copy(partner_hbm, colp.at[0], in_sem.at[1]),
    ]
    for copy in fetch:
        copy.start()

    barrier = pltpu.get_barrier_semaphore()

    ahead = 1 + (NZ - 2) * core
    for dz, flip in ((NZ - ahead, 0), (ahead, 1), (0, 1)):
        pl.semaphore_signal(
            barrier, inc=1, device_id=device(0, 0, dz, flip), device_id_type=MESH
        )
    for i in range(1, PLANE):
        pl.semaphore_signal(barrier, inc=1, device_id=plane_source(i), device_id_type=MESH)
    for copy in fetch:
        copy.wait()

    hf = feats[...].astype(F32)
    scale = lax.rsqrt(jnp.sum(hf * hf, axis=-1, keepdims=True) + 1e-06)
    embed = (hf * scale).astype(BF16)
    cols[0] = embed
    half = pl.multiple_of(core * HALF, HALF)
    rows[mine] = cols[0, pl.ds(half, HALF), :]

    pl.semaphore_wait(barrier, PLANE - 1 + 3)

    LAST = NZ // 2

    def ring_slot(k):
        if k == 0:
            return 0
        return 1 if k == LAST else 2 * k + 1 - core

    def chunk_rows(h):
        return pl.ds(pl.multiple_of((2 * core + h) % CHUNKS * CHUNK, CHUNK), CHUNK)

    def ring_copy(k, h):
        n = (k - 1) * CHUNKS + h
        target = device(0, 0, ahead, 0)
        if k == LAST:
            target = device(0, 0, ahead, h // 2)
            h = h % 2
        return remote(
            cols.at[ring_slot(k - 1), chunk_rows(h)],
            cols.at[ring_slot(k), chunk_rows(h)],
            ring_s.at[n],
            ring_r.at[n],
            target,
        )

    def pair_copy(k):
        part = cols.at[ring_slot(k)]
        return remote(part, part, pair_s.at[k - 1], pair_r.at[k - 1], device(0, 0, 0, 1))

    def mate_copy(k):
        return remote(
            colp.at[ring_slot(k - 1)],
            colp.at[ring_slot(k)],
            part_s.at[k - 1],
            part_r.at[k - 1],
            device(0, 0, ahead, 0),
        )

    def mate_pair_copy(k):
        part = colp.at[ring_slot(k)]
        return remote(part, part, part_s.at[5 + k], part_r.at[5 + k], device(0, 0, 0, 1))

    def row_copy(i):
        return remote(
            cols.at[0, pl.ds(half, HALF)], rows.at[mine], row_s.at[i], row_r.at[i], plane_dest(i)
        )

    def slot_of(off):
        off = off % NZ
        if off in (0, LAST):
            return off // LAST
        return 2 * off if off < LAST else 2 * (NZ - off) + 1

    def loop(lo, hi, act):
        def body(i, carry):
            act(i)
            return carry

        lax.fori_loop(lo, hi, body, 0)

    pending = []

    def finish():
        for settle in pending:
            settle()

    for h in range(CHUNKS):
        ring_copy(1, h).start()
    mate_copy(1).start()
    for dyi in (0, 1, 3, 2):
        for i in range(max(1, dyi * NX), dyi * NX + NX):
            row_copy(i).start()

    def settle_gather():
        for k in range(1, LAST + 1):
            for h in range(CHUNKS):
                ring_copy(k, h).wait_send()
            mate_copy(k).wait_send()
            if k < LAST:
                pair_copy(k).wait_send()
                mate_pair_copy(k).wait_send()
        loop(1, PLANE, lambda i: row_copy(i).wait_send())

    pending.append(settle_gather)

    def ring_step(k):
        for h in range(CHUNKS):
            ring_copy(k, h).wait_recv()
            if k < LAST - 1:
                ring_copy(k + 1, h).start()
            elif k == LAST - 1 and h < CHUNKS // 2:
                ring_copy(k + 1, h).start()
                ring_copy(k + 1, h + 2).start()
        mate_copy(k).wait_recv()
        if k < LAST:
            mate_copy(k + 1).start()
            pair_copy(k).start()
            mate_pair_copy(k).start()

    def pair_in(k):
        pair_copy(k).wait_recv()
        mate_pair_copy(k).wait_recv()

    def rows_in(turn):
        dyi = (NQ - turn) % NQ
        loop(max(1, dyi * NX), dyi * NX + NX, lambda i: row_copy(i).wait_recv())

    lane = lax.broadcasted_iota(jnp.int32, (1, ROWS), 1)
    row_in_tile = lax.broadcasted_iota(jnp.int32, (TILE, 1), 0)

    def row_ids(t):
        return (t * NZ * NX + z * NX) * ROWS + core * HALF + (row_in_tile // HALF) * HALF + row_in_tile

    def mates(j):
        return jnp.concatenate([colp[2 * j], colp[2 * j + 1]], axis=1)

    def score_of(t, keys):
        return lax.dot_general(
            rows[pl.ds(t * NX, NX)].reshape(TILE, WIDTH),
            keys,
            (((1,), (1,)), ((), ())),
            preferred_element_type=F32,
        ) * 10.0

    def place(slot):
        return slot - 1 if slot > 1 else slot * (NZ - 1)

    def sums(turn, slot, weight, hits):
        weight = jnp.sum(weight, axis=0, keepdims=True)
        hits = jnp.sum(hits, axis=0, keepdims=True)
        if turn == 0:
            csend[place(slot)] = weight
            ssend[place(slot)] = hits
        else:
            csend[place(slot)] += weight
            ssend[place(slot)] += hits

    def single(turn, slot):
        t = (q + turn) % NQ
        ids = row_ids(t)
        span = pl.ds(pl.multiple_of(t * TILE, TILE), TILE)
        score = score_of(t, cols[slot])
        weight = jnp.exp(score - 10.0)
        if slot == 0 and turn == 0:
            key_ids = block * ROWS + lane
            weight = jnp.where(key_ids == ids, 0.0, weight)
        hits = jnp.where(colp[slot] == ids, score, 0.0)
        ebuf[0, span, slot * ROWS : slot * ROWS + ROWS] = weight
        if slot == 0:
            dacc[span] = weight
        else:
            dacc[span] += weight
        sums(turn, slot, weight, hits)

    def pair(turn, j):
        t = (q + turn) % NQ
        ids = row_ids(t)
        span = pl.ds(pl.multiple_of(t * TILE, TILE), TILE)
        score = score_of(t, cols[2 * j : 2 * j + 2].reshape(TILE, WIDTH))
        weight = jnp.exp(score - 10.0)
        hits = jnp.where(mates(j) == ids, score, 0.0)
        ebuf[j, span] = weight
        dacc[span] += weight[:, :ROWS] + weight[:, ROWS:]
        for side in range(2):
            cut = slice(side * ROWS, side * ROWS + ROWS)
            sums(turn, 2 * j + side, weight[:, cut], hits[:, cut])

    def near_copy(i):
        return remote(
            csend.at[pl.ds(0, NEAR)],
            cmsg.at[i // 2 * 2 + core, pl.ds(0, NEAR)],
            near_s.at[i],
            near_r.at[i],
            line_dest(i),
        )

    def far_copy(i):
        return remote(
            csend.at[pl.ds(NEAR, NZ - NEAR)],
            cmsg.at[i // 2 * 2 + core, pl.ds(NEAR, NZ - NEAR)],
            far_s.at[i],
            far_r.at[i],
            line_dest(i),
        )

    ring_step(1)
    ring_step(2)
    ring_step(3)
    rows_in(0)
    single(0, 0)
    pair_in(1)
    pair(0, 1)
    pair_in(2)
    pair(0, 2)
    ring_step(4)
    rows_in(3)
    rows_in(1)
    for turn in (1, 3):
        single(turn, 0)
        pair(turn, 1)
    pair_in(3)
    pair(0, 3)
    ring_step(5)
    for turn in (1, 3):
        pair(turn, 2)
        pair(turn, 3)
    pair_in(4)
    for turn in (0, 1, 3):
        pair(turn, 4)
    rows_in(2)
    single(2, 0)
    for j in range(1, 5):
        pair(2, j)
    pair_in(5)
    for i in FAR_FIRST[2:]:
        near_copy(i).start()
    pending.append(lambda: loop(1, 2 * NZ, lambda i: near_copy(i).wait_send()))
    for turn in range(NQ):
        pair(turn, 5)
    ring_step(6)
    for i in FAR_FIRST[:2]:
        near_copy(i).start()
    for turn in range(NQ):
        single(turn, 1)

    for i in FAR_FIRST:
        far_copy(i).start()
    pending.append(lambda: loop(1, 2 * NZ, lambda i: far_copy(i).wait_send()))

    for g in range(8):
        span = pl.ds(g * ROWS, ROWS)
        rsend[pl.ds(g, 1)] = jnp.sum(dacc[span].T, axis=0, keepdims=True)

    def sum_copy(i):
        return remote(rsend, rmsg.at[mine], sum_s.at[i], sum_r.at[i], plane_dest(i))

    for dyi in (2, 1, 3, 0):
        for dx in (2, 1, 3, 0):
            if dyi + dx:
                sum_copy(dyi * NX + dx).start()
    pending.append(lambda: loop(1, PLANE, lambda i: sum_copy(i).wait_send()))

    def pos_copy(d, flip):
        n = 2 * d + flip
        return remote(
            ssend.at[place(slot_of(d))],
            smsg.at[2 * d + core],
            pos_s.at[n],
            pos_r.at[n],
            device(0, 0, d, flip),
        )

    others = [(d, flip) for d in range(NZ) for flip in range(2) if d + flip]

    rmsg[mine] = rsend[...]
    cmsg[core] = csend[...]
    smsg[core] = ssend[0]
    loop(1, PLANE, lambda i: sum_copy(i).wait_recv())
    total = rmsg[0]
    for p in range(1, PLANE):
        total = total + rmsg[p]
    square[pl.ds(0, 8)] = 1.0 / total
    turned = square[...].T
    for g in range(8):
        rrow[pl.ds(g * ROWS, ROWS)] = jnp.broadcast_to(turned[:, g : g + 1], (ROWS, ROWS))

    loop(1, 2 * NZ, lambda i: near_copy(i).wait_recv())
    loop(1, 2 * NZ, lambda i: far_copy(i).wait_recv())
    own_den = None
    for off in range(NZ):
        den = None
        for d in range(NZ):
            for c in range(2):
                part = cmsg[2 * d + c, place(slot_of(off + d))]
                den = part if den is None else den + part
        rcol[slot_of(off)] = 1.0 / den
        if off == 0:
            own_den = den
    loss_ref[...] = jnp.log(own_den) + 10.0

    def dz_copy(i):
        return remote(
            psend.at[plane_dest_slot(i)], prec.at[mine], dz_s.at[i], dz_r.at[i], plane_dest(i)
        )

    keys_all = cols[...].reshape(NZ * ROWS, WIDTH)
    for turn in (2, 1, 3, 0):
        t = (q + turn) % NQ
        ids = row_ids(t)
        span = pl.ds(pl.multiple_of(t * TILE, TILE), TILE)
        row_part = rrow[span]
        row_part = jnp.concatenate([row_part, row_part], axis=1)
        for j in range(NZ // 2):
            col_part = jnp.concatenate([rcol[2 * j], rcol[2 * j + 1]], axis=1)
            value = ebuf[j, span] * (row_part + col_part)
            value = value - jnp.where(mates(j) == ids, 2.0, 0.0)
            coeff[:, j * TILE : j * TILE + TILE] = value.astype(BF16)
        dz = jnp.dot(coeff[...], keys_all, preferred_element_type=F32)
        psend[pl.ds(t * NX, NX)] = dz.astype(BF16).reshape(NX, HALF, WIDTH)
        for dx in (2, 1, 3, 0):
            if turn + dx:
                dz_copy(turn * NX + dx).start()
    pending.append(lambda: loop(1, PLANE, lambda i: dz_copy(i).wait_send()))

    for d, flip in others:
        pos_copy(d, flip).start()
    pending.append(lambda: [pos_copy(d, flip).wait_send() for d, flip in others])
    for d, flip in others:
        pos_copy(d, flip).wait_recv()
    pos = smsg[0]
    for n in range(1, 2 * NZ):
        pos = pos + smsg[n]
    loss_ref[...] -= pos

    hf = feats[pl.ds(half, HALF)].astype(F32)
    scale = lax.rsqrt(jnp.sum(hf * hf, axis=-1, keepdims=True) + 1e-06)
    final[...] = hf * scale
    acc = psend[mine].astype(F32)
    for dyi in (2, 1, 3, 0):
        for dx in (2, 1, 3, 0):
            if dyi + dx:
                dz_copy(dyi * NX + dx).wait_recv()
                source = lax.rem(q + NQ - dyi, NQ) * NX + lax.rem(x + NX - dx, NX)
                acc = acc + prec[source].astype(F32)
    acc = acc * 10.0
    unit = final[...]
    final[...] = scale * (acc - unit * jnp.sum(unit * acc, axis=-1, keepdims=True))
    part = grad_ref.at[pl.ds(half, HALF)]
    last = remote(final, part, fin_s, fin_r, device(0, 0, 0, 1))
    last.start()
    keep = pltpu.make_async_copy(final, part, in_sem.at[0])
    keep.start()
    finish()
    keep.wait()
    last.wait()


def on_device(feats, partner):
    vmem = pl.BlockSpec(memory_space=pltpu.VMEM)
    hbm = pl.BlockSpec(memory_space=pltpu.HBM)
    dma = pltpu.SemaphoreType.DMA
    grad, loss = pl.pallas_call(
        kernel,
        out_shape=(
            jax.ShapeDtypeStruct((ROWS, WIDTH), F32),
            jax.ShapeDtypeStruct((1, ROWS), F32),
        ),
        in_specs=[hbm, hbm],
        out_specs=(hbm, vmem),
        scratch_shapes=[
            pltpu.VMEM((ROWS, WIDTH), BF16),
            pltpu.VMEM((PLANE, HALF, WIDTH), BF16),
            pltpu.VMEM((NZ, ROWS, WIDTH), BF16),
            pltpu.VMEM((NZ, 1, ROWS), jnp.int32),
            pltpu.VMEM((NZ // 2, NR, TILE), F32),
            pltpu.VMEM((NR, ROWS), F32),
            pltpu.VMEM((8, ROWS), F32),
            pltpu.VMEM((PLANE, 8, ROWS), F32),
            pltpu.VMEM((NZ, 1, ROWS), F32),
            pltpu.VMEM((2 * NZ, NZ, 1, ROWS), F32),
            pltpu.VMEM((NZ, 1, ROWS), F32),
            pltpu.VMEM((2 * NZ, 1, ROWS), F32),
            pltpu.VMEM((NZ, 1, ROWS), F32),
            pltpu.VMEM((ROWS, ROWS), F32),
            pltpu.VMEM((NR, ROWS), F32),
            pltpu.VMEM((TILE, NZ * ROWS), BF16),
            pltpu.VMEM((PLANE, HALF, WIDTH), BF16),
            pltpu.VMEM((PLANE, HALF, WIDTH), BF16),
            pltpu.VMEM((HALF, WIDTH), F32),
            dma((2,)),
        ]
        + [dma((PLANE,))] * 2
        + [dma((6 * CHUNKS,))] * 2
        + [dma((6,))] * 2
        + [dma((NZ,))] * 2
        + [dma((PLANE,))] * 2
        + [dma((2 * NZ,))] * 6
        + [dma((PLANE,))] * 2
        + [dma] * 2,
        compiler_params=pltpu.CompilerParams(
            collective_id=0, has_side_effects=True
        ),
    )(feats, partner.reshape(1, ROWS))
    return grad, loss.reshape(ROWS)


def solution(mesh):
    in_specs = (P("batch", None), P("batch"))
    out_specs = (P("batch", None), P("batch"))
    return jax.shard_map(
        on_device, mesh=mesh, in_specs=in_specs, out_specs=out_specs, check_vma=False
    )
```
